32 devices in a mesh: dp: 4 (over x, core), seq: 8 (over z, y).
Axes of the slice: x: 2, y: 2, z: 4, core: 2. Of those that a mesh axis runs over, the one named last changes fastest.
Arguments:
- spatial_input: bfloat16 [4, 8, 64, 256], P('dp', 'seq'), may hold values from -6 to 6
- temporal_input: bfloat16 [4, 64, 8, 256], P('dp', 'seq'), may hold values from -6 to 6
- out_cotangent: bfloat16 [4, 8, 64, 256], P('dp', 'seq'), may hold values from -6 to 6
- weights: bfloat16 [2, 256, 1024], replicated, may hold values from -3 to 3
- gains: float32 [2, 256], replicated, may hold values from 0.1 to 1.9
Outputs:
- input_grad: bfloat16 [4, 8, 64, 256], P('dp', 'seq')
- weight_grads: float32 [2, 262144], P(None, ('dp', 'seq'))
- gain_grads: float32 [2, 256], replicated
The draws below stay inside these ranges and needn't reach their ends.
All inputs are finite; a program needn't handle non-finite values.
Results may differ from the reference program's by a relative error of at most 0.023.
Values may be sent and summed in bfloat16 or wider, within the bound.
A program may use at most 64 MiB of HBM per device.

```python
import math
from functools import partial
import jax
import jax.numpy as jnp
from jax import lax

D = 256
HEADS = 4
FRAMES = 8
PATCHES = 64
SAMPLES = 4


def draw_weights(key, part):
    key_normal = jax.random.fold_in(jax.random.fold_in(key, 17), 0)
    drawn_cols = jax.random.truncated_normal(key_normal, -4.0, 4.0, (2, D, 4 * D), jnp.float32) * D ** (-0.5)
    return drawn_cols.astype(jnp.bfloat16)


def shard_levels(own_key, shape, cuts, smallest, largest):
    gain = 1.0
    for axis_at, blocks in cuts:
        draws = jax.random.uniform(jax.random.fold_in(jax.random.fold_in(own_key, 6), axis_at), (blocks,), jnp.float32, smallest / len(cuts), largest / len(cuts))
        gain = gain * jnp.repeat(jnp.exp(draws), shape[axis_at] // blocks).reshape((-1,) + (1,) * (len(shape) - 1 - axis_at))
    return gain


def noise(rng, extent, deviation, limit, cuts=(), dtype=jnp.bfloat16):
    array = deviation * jax.random.normal(rng, extent, jnp.float32)
    if cuts:
        array = array * shard_levels(rng, extent, cuts, -0.22, 0.18)
    return jnp.clip(array, -limit, limit).astype(dtype)


def setup_inputs(seed: int = 0) -> dict:
    splits = jax.random.split(jax.random.key(seed), 6)
    spatial_input = noise(splits[0], (SAMPLES, FRAMES, PATCHES, D), 1.0, 6.0, ((0, 4), (1, 8)))
    temporal_input = noise(splits[1], (SAMPLES, PATCHES, FRAMES, D), 1.0, 6.0, ((0, 4), (1, 8)))
    out_cotangent = noise(splits[2], (SAMPLES, FRAMES, PATCHES, D), 1.0, 6.0, ((0, 4), (1, 8)))
    weights = draw_weights(jax.random.fold_in(splits[5], 71), 0)
    gains = jnp.clip(1.0 + 0.18 * jax.random.normal(splits[4], (2, D), jnp.float32), 0.1, 1.9)
    return dict(spatial_input=spatial_input, temporal_input=temporal_input, out_cotangent=out_cotangent, weights=weights, gains=gains)


def one_head(head_parts, score_scale):
    query_rows, key_rows, value_rows = head_parts
    scores = jnp.einsum('gqe,gke->gqk', query_rows.astype(jnp.float32), key_rows.astype(jnp.float32)) * score_scale
    probs = jax.nn.softmax(scores, axis=-1).astype(jnp.bfloat16)
    return jnp.einsum('gqk,gke->gqe', probs.astype(jnp.float32), value_rows.astype(jnp.float32)).astype(jnp.bfloat16)

def attend_block(block_input, gain_vector, weight, head_count):
    groups, length, model_width = block_input.shape
    head_size = model_width // head_count
    mean_sq = lax.optimization_barrier(jnp.mean(block_input * block_input, axis=-1, keepdims=True))
    normed = (block_input * lax.rsqrt(mean_sq + 1e-06) * gain_vector).astype(jnp.bfloat16)
    w_cast = weight.astype(jnp.bfloat16)
    packed = jnp.dot(normed.reshape(groups * length, model_width), w_cast[:, :3 * model_width], preferred_element_type=jnp.float32).astype(jnp.bfloat16)
    packed = jnp.transpose(packed.reshape(groups, length, 3, head_count, head_size), (2, 3, 0, 1, 4))
    head_fn = jax.checkpoint(partial(one_head, score_scale=1.0 / math.sqrt(head_size)))
    mixed_heads = lax.map(head_fn, (packed[0], packed[1], packed[2]))
    mixed_heads = jnp.transpose(mixed_heads, (1, 2, 0, 3)).reshape(groups * length, model_width)
    result = jnp.dot(mixed_heads, w_cast[:, 3 * model_width:], preferred_element_type=jnp.float32)
    return result.reshape(groups, length, model_width)

def reference(spatial_input, temporal_input, out_cotangent, weights, gains):
    w_float = weights.astype(jnp.float32)
    block_fn = partial(attend_block, head_count=HEADS)

    def sample_grads(items):
        spatial_item, temporal_item, cot_item = items
        temporal_cot = jnp.swapaxes(cot_item, 0, 1).astype(jnp.float32)
        unused_t, pullback_t = jax.vjp(block_fn, temporal_item.astype(jnp.float32), gains[1], w_float[1])
        grad_ut, grad_gt, grad_wt = pullback_t(temporal_cot)
        mid_grad = (temporal_cot + grad_ut).astype(jnp.bfloat16)
        spatial_cot = jnp.swapaxes(mid_grad, 0, 1).astype(jnp.float32)
        unused_s, pullback_s = jax.vjp(block_fn, spatial_item.astype(jnp.float32), gains[0], w_float[0])
        grad_us, grad_gs, grad_ws = pullback_s(spatial_cot)
        in_grad = (spatial_cot + grad_us).astype(jnp.bfloat16)
        return (in_grad, jnp.stack([grad_ws, grad_wt]), jnp.stack([grad_gs, grad_gt]))
    in_grads, w_grads, g_grads = lax.map(sample_grads, (spatial_input, temporal_input, out_cotangent))
    grad_factor = 1.0 / math.sqrt(SAMPLES * FRAMES * PATCHES)
    weight_grads = (lax.optimization_barrier(jnp.sum(w_grads, axis=0)) * grad_factor).reshape(2, 4 * D * D)
    gain_grads = lax.optimization_barrier(jnp.sum(g_grads, axis=0)) * grad_factor
    return (in_grads, weight_grads, gain_grads)
```

```python
from functools import partial
import math

import jax
import jax.numpy as jnp
from jax import lax
from jax.experimental import pallas as pl
from jax.experimental.pallas import tpu as pltpu
from jax.sharding import PartitionSpec as P

HEADS = 4
F32 = jnp.float32
BF16 = jnp.bfloat16
MESH = pl.DeviceIdType.MESH


def dot(a, b, ca, cb):
    return lax.dot_general(a, b, (((ca,), (cb,)), ((), ())), preferred_element_type=F32)


def fold(x, parts):
    rows, width = x.shape
    x = x.reshape(parts, rows // parts, width)
    return jnp.concatenate([x[:, :, : width // 2], x[:, :, width // 2 :]], axis=1)


def unfold(x):
    parts, rows, half = x.shape
    x = jnp.concatenate([x[:, : rows // 2], x[:, rows // 2 :]], axis=2)
    return x.reshape(parts * (rows // 2), 2 * half)


def head_masks(rows, width):
    lane = lax.broadcasted_iota(jnp.int32, (rows, width), 1)
    size = width // HEADS
    return [(lane >= h * size) & (lane < (h + 1) * size) for h in range(HEADS)]


def spread(x, masks):
    zero = jnp.zeros_like(x)
    return jnp.concatenate([jnp.where(m, x, zero) for m in masks], axis=0)


def gather_heads(x, masks):
    rows = x.shape[0] // HEADS
    out = x[:rows]
    for h in range(1, HEADS):
        out = jnp.where(masks[h], x[h * rows : (h + 1) * rows], out)
    return out


def forward(u, gain, w_ref, block, same_group):
    rows, width = u.shape
    masks = head_masks(rows, width)
    scale = 1.0 / math.sqrt(width // HEADS)
    inv = lax.rsqrt(jnp.mean(u * u, axis=-1, keepdims=True) + 1e-06)
    unit = u * inv
    normed = (unit * gain).astype(BF16)
    packed = dot(normed, w_ref[block, :, : 3 * width], 1, 0)
    q, k, v = (packed[:, i * width : (i + 1) * width] for i in range(3))
    qs = spread(q, masks).astype(BF16)
    k = k.astype(BF16)
    v = v.astype(BF16)
    scores = dot(qs, k, 1, 1) * scale
    if same_group is not None:
        scores = jnp.where(same_group, scores, -1e30)
    e = jnp.exp(scores - jnp.max(scores, axis=-1, keepdims=True))
    probs = e / jnp.sum(e, axis=-1, keepdims=True)
    pb = probs.astype(BF16)
    mixed = gather_heads(dot(pb, v, 1, 0), masks).astype(BF16)
    return dict(unit=unit, inv=inv, normed=normed, qs=qs, k=k, v=v, probs=probs, pb=pb, mixed=mixed)


def backward_heads(cot, s, w_ref, block):
    rows, width = cot.shape
    masks = head_masks(rows, width)
    scale = 1.0 / math.sqrt(width // HEADS)
    dmixed = dot(cot, w_ref[block, :, 3 * width :], 1, 1)
    dms = spread(dmixed, masks).astype(BF16)
    dprobs = dot(dms, s["v"], 1, 1).astype(BF16).astype(F32)
    inner = jnp.sum(dprobs * s["probs"], axis=-1, keepdims=True)
    dscores = (s["probs"] * (dprobs - inner) * scale).astype(BF16)
    dq = gather_heads(dot(dscores, s["k"], 1, 0), masks)
    dk = dot(dscores, s["qs"], 0, 0)
    dv = dot(s["pb"], dms, 0, 0)
    return dq.astype(BF16), dk.astype(BF16), dv.astype(BF16)


def backward_input(dpacked, s, gain, w_ref, block):
    width = gain.shape[1]
    dn = dot(dpacked, w_ref[block, :, : 3 * width], 1, 1).astype(BF16).astype(F32)
    unit = s["unit"]
    dgain = jnp.sum(dn * unit, axis=0, keepdims=True)
    t = dn * gain
    du = s["inv"] * (t - unit * jnp.mean(unit * t, axis=-1, keepdims=True))
    return du, dgain


def weight_halves(cot, dq, dk, dv, s):
    n = s["normed"]
    left = dot(n, jnp.concatenate([dq, dk], axis=1), 0, 0)
    right = jnp.concatenate([dot(n, dv, 0, 0), dot(s["mixed"], cot, 0, 0)], axis=1)
    return left, right


def kernel(ndp, nseq, fused, factor, *refs):
    sp_ref, tp_ref, cot_ref, w_ref, g_ref = refs[:5]
    ig_ref, wg_ref, gg_ref = refs[5:8]
    csend, crecv, msend, mrecv, x_send, x_recv = refs[8:14]
    dp, seq = lax.axis_index("dp"), lax.axis_index("seq")
    rows, width = cot_ref.shape
    per = rows // nseq
    nfar = ndp // 2 * nseq
    core = lax.rem(dp, 2)
    partner = (dp + 1 - 2 * core, seq)
    me = lax.div(dp, 2) * nseq + seq

    def far(i):
        other = lax.rem(me + i, nfar)
        x = lax.div(other, nseq)
        return other, (2 * x + core, other - x * nseq)

    def near(i):
        other = lax.rem(seq + i, nseq)
        return other, (dp, other)

    barrier = pltpu.get_barrier_semaphore()
    if fused:
        pl.semaphore_signal(barrier, inc=1, device_id=partner, device_id_type=MESH)

    peer, npeer = (far, nfar) if fused else (near, nseq)

    @pl.loop(1, npeer)
    def _(i):
        pl.semaphore_signal(barrier, inc=1, device_id=peer(i)[1], device_id_type=MESH)

    def exchange(level, send, recv):
        def copy(i, slot):
            other, device = near(i)
            return pltpu.make_async_remote_copy(
                src_ref=send.at[other],
                dst_ref=recv.at[slot(other)],
                send_sem=x_send.at[level, other],
                recv_sem=x_recv.at[level, slot(other)],
                device_id=device,
                device_id_type=MESH,
            )

        def start():
            @pl.loop(1, nseq)
            def _(i):
                copy(i, lambda other: seq).start()

        def arrive():
            @pl.loop(1, nseq)
            def _(i):
                copy(i, lambda other: other).wait_recv()

        def finish():
            @pl.loop(1, nseq)
            def _(i):
                copy(i, lambda other: seq).wait_send()

        return start, arrive, finish

    c_start, c_arrive, c_finish = exchange(0, csend, crecv)
    m_start, m_arrive, m_finish = exchange(1, msend, mrecv)

    csend[...] = fold(cot_ref[...].astype(F32), nseq).astype(BF16)
    crecv[seq] = csend[seq]

    frames = rows // per
    at = lax.broadcasted_iota(jnp.int32, (rows, rows), 0)
    frm = lax.broadcasted_iota(jnp.int32, (rows, rows), 1)
    pick = (frm == lax.rem(at, per) * frames + lax.div(at, per)).astype(F32).astype(BF16)
    ut = dot(pick, tp_ref[...], 1, 0)
    ri = lax.broadcasted_iota(jnp.int32, (HEADS * rows, rows), 0)
    ci = lax.broadcasted_iota(jnp.int32, (HEADS * rows, rows), 1)
    same = lax.rem(ri, per) == lax.rem(ci, per)
    g_t, g_s = g_ref[1:2, :], g_ref[0:1, :]
    st = forward(ut, g_t, w_ref, 1, same)

    pl.semaphore_wait(barrier, npeer if fused else npeer - 1)
    c_start()
    ss = forward(sp_ref[...].astype(F32), g_s, w_ref, 0, None)
    c_arrive()

    if fused:
        part, arecv, bsend, brecv, gown, garecv, gbsend, gbrecv = refs[14:22]
        a_send, a_recv, b_send, b_recv = refs[22:26]
        chunk = part.shape[3]

        def near_copy(level, src, dst):
            return pltpu.make_async_remote_copy(
                src_ref=src,
                dst_ref=dst,
                send_sem=a_send.at[level],
                recv_sem=a_recv.at[level],
                device_id=partner,
                device_id_type=MESH,
            )

        a_copies = [near_copy(b, part.at[b, 1 - core], arecv.at[b]) for b in range(2)]
        a_copies.append(near_copy(2, gown, garecv))

        def far_copy(level, i, sending):
            other, device = far(i)
            slot = me if sending else other
            if level == 2:
                src, dst = gbsend, gbrecv.at[slot]
            else:
                src, dst = bsend.at[level, other], brecv.at[level, slot]
            return pltpu.make_async_remote_copy(
                src_ref=src,
                dst_ref=dst,
                send_sem=b_send.at[level, other],
                recv_sem=b_recv.at[level, slot],
                device_id=device,
                device_id_type=MESH,
            )

        def put_weights(b, left, right):
            both = jnp.concatenate(
                [left.reshape(2 * nfar, chunk // 2, -1), right.reshape(2 * nfar, chunk // 2, -1)],
                axis=1,
            ).astype(BF16)
            both = both.reshape(ndp // 2, 2, nseq, chunk, -1)
            for c in range(2):
                part[b, c] = both[:, c].reshape(nfar, chunk, -1)
            a_copies[b].start()

        def far_start(b):
            a_copies[b].wait_recv()
            total = part[b, core].astype(F32) + arecv[b].astype(F32)
            bsend[b] = total.astype(BF16)
            brecv[b, me] = bsend[b, me]

            @pl.loop(1, nfar)
            def _(i):
                far_copy(b, i, True).start()

        def far_end(b):
            @pl.loop(1, nfar)
            def _(i):
                far_copy(b, i, False).wait_recv()

            total = jnp.sum(brecv[b].astype(F32), axis=0) * factor
            r = chunk // 2
            half = total.shape[1]
            for i in range(r):
                wg_ref[b : b + 1, 2 * i * half : (2 * i + 1) * half] = total[i : i + 1]
                wg_ref[b : b + 1, (2 * i + 1) * half : (2 * i + 2) * half] = total[r + i : r + i + 1]
    else:

        def put_weights(b, left, right):
            w = left.shape[1]
            wg_ref[b, :, :w] = (left * factor).astype(BF16)
            wg_ref[b, :, w:] = (right * factor).astype(BF16)

    cot_t = unfold(crecv[...].astype(F32))
    cot_tb = cot_t.astype(BF16)
    dq, dk, dv = backward_heads(cot_tb, st, w_ref, 1)
    du, dg_t = backward_input(jnp.concatenate([dq, dk, dv], axis=1), st, g_t, w_ref, 1)
    msend[...] = fold(cot_t + du, nseq).astype(BF16)
    mrecv[seq] = msend[seq]
    m_start()
    put_weights(1, *weight_halves(cot_tb, dq, dk, dv, st))

    m_arrive()
    cot_s = unfold(mrecv[...].astype(F32))
    cot_sb = cot_s.astype(BF16)
    if fused:
        far_start(1)
    dq, dk, dv = backward_heads(cot_sb, ss, w_ref, 0)
    put_weights(0, *weight_halves(cot_sb, dq, dk, dv, ss))
    du, dg_s = backward_input(jnp.concatenate([dq, dk, dv], axis=1), ss, g_s, w_ref, 0)
    ig_ref[...] = (cot_s + du).astype(BF16)

    if fused:
        gown[...] = jnp.zeros_like(gown)
        gown[0:1, :] = dg_s
        gown[1:2, :] = dg_t
        a_copies[2].start()
        far_start(0)
        a_copies[2].wait_recv()
        gbsend[...] = gown[...] + garecv[...]
        gbrecv[me] = gbsend[...]

        @pl.loop(1, nfar)
        def _(i):
            far_copy(2, i, True).start()

        far_end(1)
        far_end(0)

        @pl.loop(1, nfar)
        def _(i):
            far_copy(2, i, False).wait_recv()

        gg_ref[...] = jnp.sum(gbrecv[...], axis=0)[0:2] * factor
        for c in a_copies:
            c.wait_send()
        for level in range(3):

            @pl.loop(1, nfar)
            def _(i):
                far_copy(level, i, True).wait_send()
    else:
        gg_ref[0:1, :] = dg_s * factor
        gg_ref[1:2, :] = dg_t * factor
    c_finish()
    m_finish()


def per_device(spatial_input, temporal_input, out_cotangent, weights, gains):
    ndp, nseq = lax.axis_size("dp"), lax.axis_size("seq")
    width = spatial_input.shape[-1]
    rows = spatial_input.shape[1] * spatial_input.shape[2]
    factor = 1.0 / math.sqrt(spatial_input.shape[0] * ndp * nseq * rows)
    per = rows // nseq
    wide = weights.shape[2]
    chunk_rows = width // (ndp * nseq)
    fused = ndp % 2 == 0 and chunk_rows * ndp * nseq == width and chunk_rows % 8 == 0
    nfar = ndp // 2 * nseq
    message = pltpu.VMEM((nseq, 2 * per, width // 2), BF16)
    scratch = [message] * 4 + [pltpu.SemaphoreType.DMA((2, nseq))] * 2
    if fused:
        block = (2 * chunk_rows, wide // 2)
        scratch += [
            pltpu.VMEM((2, 2, nfar) + block, BF16),
            pltpu.VMEM((2, nfar) + block, BF16),
            pltpu.VMEM((2, nfar) + block, BF16),
            pltpu.VMEM((2, nfar) + block, BF16),
            pltpu.VMEM((8, width), F32),
            pltpu.VMEM((8, width), F32),
            pltpu.VMEM((8, width), F32),
            pltpu.VMEM((nfar, 8, width), F32),
            pltpu.SemaphoreType.DMA((3,)),
            pltpu.SemaphoreType.DMA((3,)),
            pltpu.SemaphoreType.DMA((3, nfar)),
            pltpu.SemaphoreType.DMA((3, nfar)),
        ]
        wg_shape = jax.ShapeDtypeStruct((2, chunk_rows * wide), F32)
    else:
        wg_shape = jax.ShapeDtypeStruct((2, width, wide), BF16)
    vmem = pl.BlockSpec(memory_space=pltpu.VMEM)
    input_grad, weight_grads, gain_grads = pl.pallas_call(
        partial(kernel, ndp, nseq, fused, factor),
        out_shape=(
            jax.ShapeDtypeStruct((rows, width), BF16),
            wg_shape,
            jax.ShapeDtypeStruct((2, width), F32),
        ),
        in_specs=[vmem] * 5,
        out_specs=(vmem,) * 3,
        scratch_shapes=scratch,
        compiler_params=pltpu.CompilerParams(
            collective_id=0, has_side_effects=True, vmem_limit_bytes=48 * 1024 * 1024
        ),
    )(
        spatial_input.reshape(rows, width),
        temporal_input.reshape(rows, width),
        out_cotangent.reshape(rows, width),
        weights,
        gains,
    )
    if not fused:
        grid = weight_grads.reshape(2, ndp, nseq, -1)
        over = lax.psum_scatter(grid, "seq", scatter_dimension=2, tiled=True)
        over = lax.psum_scatter(
            over.reshape(2, ndp, -1), "dp", scatter_dimension=1, tiled=True
        )
        weight_grads = over.astype(F32).reshape(2, -1)
        gain_grads = lax.psum(gain_grads, ("dp", "seq"))
    return input_grad.reshape(spatial_input.shape), weight_grads, gain_grads


def solution(mesh):
    return jax.shard_map(
        per_device,
        mesh=mesh,
        in_specs=(
            P("dp", "seq", None, None),
            P("dp", "seq", None, None),
            P("dp", "seq", None, None),
            P(),
            P(),
        ),
        out_specs=(P("dp", "seq", None, None), P(None, ("dp", "seq")), P()),
        check_vma=False,
    )
```

```python
from functools import partial
import math

import jax
import jax.numpy as jnp
from jax import lax
from jax.experimental import pallas as pl
from jax.experimental.pallas import tpu as pltpu
from jax.sharding import PartitionSpec as P

HEADS = 4
F32 = jnp.float32
BF16 = jnp.bfloat16
MESH = pl.DeviceIdType.MESH


def dot(a, b, ca, cb):
    return lax.dot_general(a, b, (((ca,), (cb,)), ((), ())), preferred_element_type=F32)


def fold(x, parts):
    rows, width = x.shape
    x = x.reshape(parts, rows // parts, width)
    return jnp.concatenate([x[:, :, : width // 2], x[:, :, width // 2 :]], axis=1)


def unfold(x):
    parts, rows, half = x.shape
    x = jnp.concatenate([x[:, : rows // 2], x[:, rows // 2 :]], axis=2)
    return x.reshape(parts * (rows // 2), 2 * half)


def head_masks(rows, width):
    lane = lax.broadcasted_iota(jnp.int32, (rows, width), 1)
    size = width // HEADS
    return [(lane >= h * size) & (lane < (h + 1) * size) for h in range(HEADS)]


def spread(x, masks):
    zero = jnp.zeros_like(x)
    return jnp.concatenate([jnp.where(m, x, zero) for m in masks], axis=0)


def gather_heads(x, masks):
    rows = x.shape[0] // HEADS
    out = x[:rows]
    for h in range(1, HEADS):
        out = jnp.where(masks[h], x[h * rows : (h + 1) * rows], out)
    return out


def forward(u, gain, w_ref, block, same_group):
    rows, width = u.shape
    masks = head_masks(rows, width)
    scale = 1.0 / math.sqrt(width // HEADS)
    inv = lax.rsqrt(jnp.mean(u * u, axis=-1, keepdims=True) + 1e-06)
    unit = u * inv
    normed = (unit * gain).astype(BF16)
    packed = dot(normed, w_ref[block, :, : 3 * width], 1, 0)
    q, k, v = (packed[:, i * width : (i + 1) * width] for i in range(3))
    qs = spread(q, masks).astype(BF16)
    k = k.astype(BF16)
    v = v.astype(BF16)
    scores = dot(qs, k, 1, 1) * scale
    if same_group is not None:
        scores = jnp.where(same_group, scores, -1e30)
    e = jnp.exp(scores - jnp.max(scores, axis=-1, keepdims=True))
    probs = e / jnp.sum(e, axis=-1, keepdims=True)
    pb = probs.astype(BF16)
    mixed = gather_heads(dot(pb, v, 1, 0), masks).astype(BF16)
    return dict(unit=unit, inv=inv, normed=normed, qs=qs, k=k, v=v, probs=probs, pb=pb, mixed=mixed)


def backward_heads(cot, s, w_ref, block):
    rows, width = cot.shape
    masks = head_masks(rows, width)
    scale = 1.0 / math.sqrt(width // HEADS)
    dmixed = dot(cot, w_ref[block, :, 3 * width :], 1, 1)
    dms = spread(dmixed, masks).astype(BF16)
    dprobs = dot(dms, s["v"], 1, 1).astype(BF16).astype(F32)
    inner = jnp.sum(dprobs * s["probs"], axis=-1, keepdims=True)
    dscores = (s["probs"] * (dprobs - inner) * scale).astype(BF16)
    dq = gather_heads(dot(dscores, s["k"], 1, 0), masks)
    dk = dot(dscores, s["qs"], 0, 0)
    dv = dot(s["pb"], dms, 0, 0)
    return dq.astype(BF16), dk.astype(BF16), dv.astype(BF16)


def backward_input(dpacked, s, gain, w_ref, block):
    width = gain.shape[1]
    dn = dot(dpacked, w_ref[block, :, : 3 * width], 1, 1).astype(BF16).astype(F32)
    unit = s["unit"]
    dgain = jnp.sum(dn * unit, axis=0, keepdims=True)
    t = dn * gain
    du = s["inv"] * (t - unit * jnp.mean(unit * t, axis=-1, keepdims=True))
    return du, dgain


def weight_halves(cot, dq, dk, dv, s):
    n = s["normed"]
    left = dot(n, jnp.concatenate([dq, dk], axis=1), 0, 0)
    right = jnp.concatenate([dot(n, dv, 0, 0), dot(s["mixed"], cot, 0, 0)], axis=1)
    return left, right


def kernel(ndp, nseq, fused, factor, *refs):
    ig_ref, wg_ref, gg_ref = refs[5:8]
    sp_ref, tp_ref, cot_ref, w_ref, g_ref, load_sem = refs[8:14]
    csend, crecv, msend, mrecv, x_send, x_recv = refs[14:20]
    sp_hbm, tp_hbm, cot_hbm, w_hbm, g_hbm = refs[:5]
    pairs = [
        (cot_hbm, cot_ref),
        (tp_hbm, tp_ref),
        (g_hbm, g_ref),
        (w_hbm.at[1], w_ref.at[1]),
        (sp_hbm, sp_ref),
        (w_hbm.at[0], w_ref.at[0]),
    ]
    loads = [pltpu.make_async_copy(s, d, load_sem.at[i]) for i, (s, d) in enumerate(pairs)]
    for load in loads:
        load.start()
    dp, seq = lax.axis_index("dp"), lax.axis_index("seq")
    rows, width = cot_ref.shape
    per = rows // nseq
    nfar = ndp // 2 * nseq
    core = lax.rem(dp, 2)
    partner = (dp + 1 - 2 * core, seq)
    me = lax.div(dp, 2) * nseq + seq

    def far(i):
        other = lax.rem(me + i, nfar)
        x = lax.div(other, nseq)
        return other, (2 * x + core, other - x * nseq)

    def near(i):
        other = lax.rem(seq + i, nseq)
        return other, (dp, other)

    barrier = pltpu.get_barrier_semaphore()
    if fused:
        pl.semaphore_signal(barrier, inc=1, device_id=partner, device_id_type=MESH)

    peer, npeer = (far, nfar) if fused else (near, nseq)

    @pl.loop(1, npeer)
    def _(i):
        pl.semaphore_signal(barrier, inc=1, device_id=peer(i)[1], device_id_type=MESH)

    def exchange(level, send, recv):
        def copy(i, slot):
            other, device = near(i)
            return pltpu.make_async_remote_copy(
                src_ref=send.at[other],
                dst_ref=recv.at[slot(other)],
                send_sem=x_send.at[level, other],
                recv_sem=x_recv.at[level, slot(other)],
                device_id=device,
                device_id_type=MESH,
            )

        def start():
            @pl.loop(1, nseq)
            def _(i):
                copy(i, lambda other: seq).start()

        def arrive():
            @pl.loop(1, nseq)
            def _(i):
                copy(i, lambda other: other).wait_recv()

        def finish():
            @pl.loop(1, nseq)
            def _(i):
                copy(i, lambda other: seq).wait_send()

        return start, arrive, finish

    c_start, c_arrive, c_finish = exchange(0, csend, crecv)
    m_start, m_arrive, m_finish = exchange(1, msend, mrecv)

    loads[0].wait()
    csend[...] = fold(cot_ref[...].astype(F32), nseq).astype(BF16)
    crecv[seq] = csend[seq]

    frames = rows // per
    at = lax.broadcasted_iota(jnp.int32, (rows, rows), 0)
    frm = lax.broadcasted_iota(jnp.int32, (rows, rows), 1)
    pick = (frm == lax.rem(at, per) * frames + lax.div(at, per)).astype(F32).astype(BF16)
    loads[1].wait()
    ut = dot(pick, tp_ref[...], 1, 0)
    ri = lax.broadcasted_iota(jnp.int32, (HEADS * rows, rows), 0)
    ci = lax.broadcasted_iota(jnp.int32, (HEADS * rows, rows), 1)
    same = lax.rem(ri, per) == lax.rem(ci, per)
    loads[2].wait()
    loads[3].wait()
    g_t, g_s = g_ref[1:2, :], g_ref[0:1, :]
    st = forward(ut, g_t, w_ref, 1, same)

    pl.semaphore_wait(barrier, npeer if fused else npeer - 1)
    c_start()
    loads[4].wait()
    loads[5].wait()
    ss = forward(sp_ref[...].astype(F32), g_s, w_ref, 0, None)
    c_arrive()

    if fused:
        part, arecv, bsend, brecv, gown, garecv, gbsend, gbrecv = refs[20:28]
        a_send, a_recv, b_send, b_recv = refs[28:32]
        chunk = part.shape[3]

        def near_copy(level, src, dst):
            return pltpu.make_async_remote_copy(
                src_ref=src,
                dst_ref=dst,
                send_sem=a_send.at[level],
                recv_sem=a_recv.at[level],
                device_id=partner,
                device_id_type=MESH,
            )

        a_copies = [near_copy(b, part.at[b, 1 - core], arecv.at[b]) for b in range(2)]
        a_copies.append(near_copy(2, gown, garecv))

        def far_copy(level, i, sending):
            other, device = far(i)
            slot = me if sending else other
            if level == 2:
                src, dst = gbsend, gbrecv.at[slot]
            else:
                src, dst = bsend.at[level, other], brecv.at[level, slot]
            return pltpu.make_async_remote_copy(
                src_ref=src,
                dst_ref=dst,
                send_sem=b_send.at[level, other],
                recv_sem=b_recv.at[level, slot],
                device_id=device,
                device_id_type=MESH,
            )

        def put_weights(b, left, right):
            both = jnp.concatenate(
                [left.reshape(2 * nfar, chunk // 2, -1), right.reshape(2 * nfar, chunk // 2, -1)],
                axis=1,
            ).astype(BF16)
            both = both.reshape(ndp // 2, 2, nseq, chunk, -1)
            for c in range(2):
                part[b, c] = both[:, c].reshape(nfar, chunk, -1)
            a_copies[b].start()

        def far_start(b):
            a_copies[b].wait_recv()
            total = part[b, core].astype(F32) + arecv[b].astype(F32)
            bsend[b] = total.astype(BF16)
            brecv[b, me] = bsend[b, me]

            @pl.loop(1, nfar)
            def _(i):
                far_copy(b, i, True).start()

        def far_end(b):
            @pl.loop(1, nfar)
            def _(i):
                far_copy(b, i, False).wait_recv()

            total = jnp.sum(brecv[b].astype(F32), axis=0) * factor
            r = chunk // 2
            half = total.shape[1]
            for i in range(r):
                wg_ref[b : b + 1, 2 * i * half : (2 * i + 1) * half] = total[i : i + 1]
                wg_ref[b : b + 1, (2 * i + 1) * half : (2 * i + 2) * half] = total[r + i : r + i + 1]
    else:

        def put_weights(b, left, right):
            w = left.shape[1]
            wg_ref[b, :, :w] = (left * factor).astype(BF16)
            wg_ref[b, :, w:] = (right * factor).astype(BF16)

    cot_t = unfold(crecv[...].astype(F32))
    cot_tb = cot_t.astype(BF16)
    dq, dk, dv = backward_heads(cot_tb, st, w_ref, 1)
    du, dg_t = backward_input(jnp.concatenate([dq, dk, dv], axis=1), st, g_t, w_ref, 1)
    msend[...] = fold(cot_t + du, nseq).astype(BF16)
    mrecv[seq] = msend[seq]
    m_start()
    put_weights(1, *weight_halves(cot_tb, dq, dk, dv, st))

    m_arrive()
    cot_s = unfold(mrecv[...].astype(F32))
    cot_sb = cot_s.astype(BF16)
    if fused:
        far_start(1)
    dq, dk, dv = backward_heads(cot_sb, ss, w_ref, 0)
    put_weights(0, *weight_halves(cot_sb, dq, dk, dv, ss))
    du, dg_s = backward_input(jnp.concatenate([dq, dk, dv], axis=1), ss, g_s, w_ref, 0)
    ig_ref[...] = (cot_s + du).astype(BF16)

    if fused:
        gown[...] = jnp.zeros_like(gown)
        gown[0:1, :] = dg_s
        gown[1:2, :] = dg_t
        a_copies[2].start()
        far_start(0)
        a_copies[2].wait_recv()
        gbsend[...] = gown[...] + garecv[...]
        gbrecv[me] = gbsend[...]

        @pl.loop(1, nfar)
        def _(i):
            far_copy(2, i, True).start()

        far_end(1)
        far_end(0)

        @pl.loop(1, nfar)
        def _(i):
            far_copy(2, i, False).wait_recv()

        gg_ref[...] = jnp.sum(gbrecv[...], axis=0)[0:2] * factor
        for c in a_copies:
            c.wait_send()
        for level in range(3):

            @pl.loop(1, nfar)
            def _(i):
                far_copy(level, i, True).wait_send()
    else:
        gg_ref[0:1, :] = dg_s * factor
        gg_ref[1:2, :] = dg_t * factor
    c_finish()
    m_finish()


def store_kernel(*refs):
    n = len(refs) // 2
    sem = refs[-1]
    copies = [pltpu.make_async_copy(refs[i], refs[n + i], sem.at[i]) for i in range(n)]
    for c in copies:
        c.start()
    for c in copies:
        c.wait()


def store_results(results):
    n = len(results)
    return pl.pallas_call(
        store_kernel,
        out_shape=tuple(jax.ShapeDtypeStruct(r.shape, r.dtype) for r in results),
        in_specs=[pl.BlockSpec(memory_space=pl.ANY)] * n,
        out_specs=(pl.BlockSpec(memory_space=pltpu.HBM),) * n,
        scratch_shapes=[pltpu.SemaphoreType.DMA((n,))],
        compiler_params=pltpu.CompilerParams(vmem_limit_bytes=1024 * 1024),
    )(*results)


def per_device(spatial_input, temporal_input, out_cotangent, weights, gains):
    ndp, nseq = lax.axis_size("dp"), lax.axis_size("seq")
    width = spatial_input.shape[-1]
    rows = spatial_input.shape[1] * spatial_input.shape[2]
    factor = 1.0 / math.sqrt(spatial_input.shape[0] * ndp * nseq * rows)
    per = rows // nseq
    wide = weights.shape[2]
    chunk_rows = width // (ndp * nseq)
    fused = ndp % 2 == 0 and chunk_rows * ndp * nseq == width and chunk_rows % 8 == 0
    nfar = ndp // 2 * nseq
    message = pltpu.VMEM((nseq, 2 * per, width // 2), BF16)
    args = (
        spatial_input.reshape(rows, width),
        temporal_input.reshape(rows, width),
        out_cotangent.reshape(rows, width),
        weights,
        gains,
    )
    scratch = [pltpu.VMEM(a.shape, a.dtype) for a in args] + [pltpu.SemaphoreType.DMA((6,))]
    scratch += [message] * 4 + [pltpu.SemaphoreType.DMA((2, nseq))] * 2
    if fused:
        block = (2 * chunk_rows, wide // 2)
        scratch += [
            pltpu.VMEM((2, 2, nfar) + block, BF16),
            pltpu.VMEM((2, nfar) + block, BF16),
            pltpu.VMEM((2, nfar) + block, BF16),
            pltpu.VMEM((2, nfar) + block, BF16),
            pltpu.VMEM((8, width), F32),
            pltpu.VMEM((8, width), F32),
            pltpu.VMEM((8, width), F32),
            pltpu.VMEM((nfar, 8, width), F32),
            pltpu.SemaphoreType.DMA((3,)),
            pltpu.SemaphoreType.DMA((3,)),
            pltpu.SemaphoreType.DMA((3, nfar)),
            pltpu.SemaphoreType.DMA((3, nfar)),
        ]
        wg_shape = jax.ShapeDtypeStruct((2, chunk_rows * wide), F32)
    else:
        wg_shape = jax.ShapeDtypeStruct((2, width, wide), BF16)
    vmem = pl.BlockSpec(memory_space=pltpu.VMEM)
    results = pl.pallas_call(
        partial(kernel, ndp, nseq, fused, factor),
        out_shape=(
            jax.ShapeDtypeStruct((rows, width), BF16),
            wg_shape,
            jax.ShapeDtypeStruct((2, width), F32),
        ),
        in_specs=[pl.BlockSpec(memory_space=pltpu.HBM)] * 5,
        out_specs=(vmem,) * 3,
        scratch_shapes=scratch,
        compiler_params=pltpu.CompilerParams(
            collective_id=0, has_side_effects=True, vmem_limit_bytes=48 * 1024 * 1024
        ),
    )(*[pltpu.with_memory_space_constraint(a, pltpu.HBM) for a in args])
    input_grad, weight_grads, gain_grads = store_results(results) if fused else results
    if not fused:
        grid = weight_grads.reshape(2, ndp, nseq, -1)
        over = lax.psum_scatter(grid, "seq", scatter_dimension=2, tiled=True)
        over = lax.psum_scatter(
            over.reshape(2, ndp, -1), "dp", scatter_dimension=1, tiled=True
        )
        weight_grads = over.astype(F32).reshape(2, -1)
        gain_grads = lax.psum(gain_grads, ("dp", "seq"))
    return input_grad.reshape(spatial_input.shape), weight_grads, gain_grads


def solution(mesh):
    return jax.shard_map(
        per_device,
        mesh=mesh,
        in_specs=(
            P("dp", "seq", None, None),
            P("dp", "seq", None, None),
            P("dp", "seq", None, None),
            P(),
            P(),
        ),
        out_specs=(P("dp", "seq", None, None), P(None, ("dp", "seq")), P()),
        check_vma=False,
    )
```

```python
from functools import partial
import math

import jax
import jax.numpy as jnp
from jax import lax
from jax.experimental import pallas as pl
from jax.experimental.pallas import tpu as pltpu
from jax.sharding import PartitionSpec as P

HEADS = 4
F32 = jnp.float32
BF16 = jnp.bfloat16
MESH = pl.DeviceIdType.MESH


def dot(a, b, ca, cb):
    return lax.dot_general(a, b, (((ca,), (cb,)), ((), ())), preferred_element_type=F32)


def fold(x, parts):
    rows, width = x.shape
    x = x.reshape(parts, rows // parts, width)
    return jnp.concatenate([x[:, :, : width // 2], x[:, :, width // 2 :]], axis=1)


def unfold(x):
    parts, rows, half = x.shape
    x = jnp.concatenate([x[:, : rows // 2], x[:, rows // 2 :]], axis=2)
    return x.reshape(parts * (rows // 2), 2 * half)


def head_masks(rows, width):
    lane = lax.broadcasted_iota(jnp.int32, (rows, width), 1)
    size = width // HEADS
    return [(lane >= h * size) & (lane < (h + 1) * size) for h in range(HEADS)]


def spread(x, masks):
    zero = jnp.zeros_like(x)
    return jnp.concatenate([jnp.where(m, x, zero) for m in masks], axis=0)


def gather_heads(x, masks):
    rows = x.shape[0] // HEADS
    out = x[:rows]
    for h in range(1, HEADS):
        out = jnp.where(masks[h], x[h * rows : (h + 1) * rows], out)
    return out


def forward(u, gain, w_ref, block, same_group):
    rows, width = u.shape
    masks = head_masks(rows, width)
    scale = 1.0 / math.sqrt(width // HEADS)
    inv = lax.rsqrt(jnp.mean(u * u, axis=-1, keepdims=True) + 1e-06)
    unit = u * inv
    normed = (unit * gain).astype(BF16)
    packed = dot(normed, w_ref[block, :, : 3 * width], 1, 0)
    q, k, v = (packed[:, i * width : (i + 1) * width] for i in range(3))
    qs = spread(q, masks).astype(BF16)
    k = k.astype(BF16)
    v = v.astype(BF16)
    scores = dot(qs, k, 1, 1) * scale
    if same_group is not None:
        scores = jnp.where(same_group, scores, -1e30)
    e = jnp.exp(scores - jnp.max(scores, axis=-1, keepdims=True))
    probs = e / jnp.sum(e, axis=-1, keepdims=True)
    pb = probs.astype(BF16)
    mixed = gather_heads(dot(pb, v, 1, 0), masks).astype(BF16)
    return dict(unit=unit, inv=inv, normed=normed, qs=qs, k=k, v=v, probs=probs, pb=pb, mixed=mixed)


def backward_value(cot, s, w_ref, block):
    rows, width = cot.shape
    dmixed = dot(cot, w_ref[block, :, 3 * width :], 1, 1)
    dms = spread(dmixed, head_masks(rows, width)).astype(BF16)
    return dms, dot(s["pb"], dms, 0, 0).astype(BF16)


def backward_scores(dms, s):
    rows, width = s["k"].shape
    scale = 1.0 / math.sqrt(width // HEADS)
    dprobs = dot(dms, s["v"], 1, 1).astype(BF16).astype(F32)
    inner = jnp.sum(dprobs * s["probs"], axis=-1, keepdims=True)
    dscores = (s["probs"] * (dprobs - inner) * scale).astype(BF16)
    dq = gather_heads(dot(dscores, s["k"], 1, 0), head_masks(rows, width))
    dk = dot(dscores, s["qs"], 0, 0)
    return dq.astype(BF16), dk.astype(BF16)


def backward_input(dpacked, s, gain, w_ref, block):
    width = gain.shape[1]
    dn = dot(dpacked, w_ref[block, :, : 3 * width], 1, 1).astype(BF16).astype(F32)
    unit = s["unit"]
    dgain = jnp.sum(dn * unit, axis=0, keepdims=True)
    t = dn * gain
    du = s["inv"] * (t - unit * jnp.mean(unit * t, axis=-1, keepdims=True))
    return du, dgain


def each(n, body):
    if n <= 9:
        for i in range(1, n):
            body(i)
    else:
        pl.loop(1, n)(body)


def groups(ndp, nseq):
    inner = 2 if nseq % 2 == 0 else 1
    return inner, ndp // 2 * inner, nseq // inner


def kernel(ndp, nseq, fused, factor, *refs):
    ig_ref, wg_ref, gg_ref = refs[5:8]
    sp_ref, tp_ref, cot_ref, w_ref, g_ref, load_sem = refs[8:14]
    csend, crecv, msend, mrecv, x_send, x_recv = refs[14:20]
    sp_hbm, tp_hbm, cot_hbm, w_hbm, g_hbm = refs[:5]
    pairs = [
        (cot_hbm, cot_ref),
        (tp_hbm, tp_ref),
        (g_hbm, g_ref),
        (w_hbm.at[1], w_ref.at[1]),
        (sp_hbm, sp_ref),
        (w_hbm.at[0], w_ref.at[0]),
    ]
    loads = [pltpu.make_async_copy(s, d, load_sem.at[i]) for i, (s, d) in enumerate(pairs)]
    for load in loads:
        load.start()
    dp, seq = lax.axis_index("dp"), lax.axis_index("seq")
    rows, width = cot_ref.shape
    per = rows // nseq
    inner, n1, n2 = groups(ndp, nseq)
    core = lax.rem(dp, 2)
    partner = (dp + 1 - 2 * core, seq)
    far = lax.div(dp, 2)
    z = lax.div(seq, inner)
    y = seq - z * inner
    me = (far * inner + y, z)

    def peer1(i):
        other = lax.rem(me[0] + i, n1)
        x = lax.div(other, inner)
        return other, (2 * x + core, z * inner + other - x * inner)

    def peer2(i):
        other = lax.rem(z + i, n2)
        return other, (dp, other * inner + y)

    def near(i):
        other = lax.rem(seq + i, nseq)
        return other, (dp, other)

    barrier = pltpu.get_barrier_semaphore()

    def greet(device):
        pl.semaphore_signal(barrier, inc=1, device_id=device, device_id_type=MESH)

    each(nseq, lambda i: greet(near(i)[1]))
    greeted = nseq - 1
    if fused:
        greet(partner)
        nx = ndp // 2
        for k in range(inner):
            each(nx, lambda i: greet((2 * lax.rem(far + i, nx) + core, z * inner + k)))
        greeted += 1 + inner * (nx - 1)

    def exchange(level, send, recv):
        def copy(i, slot):
            other, device = near(i)
            return pltpu.make_async_remote_copy(
                src_ref=send.at[other],
                dst_ref=recv.at[slot(other)],
                send_sem=x_send.at[level, other],
                recv_sem=x_recv.at[level, slot(other)],
                device_id=device,
                device_id_type=MESH,
            )

        def start():
            each(nseq, lambda i: copy(i, lambda other: seq).start())

        def arrive():
            each(nseq, lambda i: copy(i, lambda other: other).wait_recv())

        def finish():
            each(nseq, lambda i: copy(i, lambda other: seq).wait_send())

        return start, arrive, finish

    c_start, c_arrive, c_finish = exchange(0, csend, crecv)
    m_start, m_arrive, m_finish = exchange(1, msend, mrecv)

    loads[0].wait()
    csend[...] = fold(cot_ref[...].astype(F32), nseq).astype(BF16)
    crecv[seq] = csend[seq]

    frames = rows // per
    at = lax.broadcasted_iota(jnp.int32, (rows, rows), 0)
    frm = lax.broadcasted_iota(jnp.int32, (rows, rows), 1)
    pick = (frm == lax.rem(at, per) * frames + lax.div(at, per)).astype(F32).astype(BF16)
    loads[1].wait()
    ut = dot(pick, tp_ref[...], 1, 0)
    ri = lax.broadcasted_iota(jnp.int32, (HEADS * rows, rows), 0)
    ci = lax.broadcasted_iota(jnp.int32, (HEADS * rows, rows), 1)
    same = lax.rem(ri, per) == lax.rem(ci, per)
    loads[2].wait()
    loads[3].wait()
    g_t, g_s = g_ref[1:2, :], g_ref[0:1, :]
    st = forward(ut, g_t, w_ref, 1, same)

    pl.semaphore_wait(barrier, greeted)
    c_start()
    loads[4].wait()
    loads[5].wait()
    ss = forward(sp_ref[...].astype(F32), g_s, w_ref, 0, None)
    c_arrive()

    if fused:
        part, arecv, send1, recv1, send2, recv2 = refs[20:26]
        gown, garecv, gsend1, grecv1, gsend2, grecv2 = refs[26:32]
        a_send, a_recv, s_send1, s_recv1, s_send2, s_recv2 = refs[32:38]
        chunk = part.shape[4]
        sends = (send1, send2)
        recvs = (recv1, recv2)
        gsends = (gsend1, gsend2)
        grecvs = (grecv1, grecv2)
        send_sems = (s_send1, s_send2)
        recv_sems = (s_recv1, s_recv2)
        peers = (peer1, peer2)
        sizes = (n1, n2)

        a_copies = [
            pltpu.make_async_remote_copy(
                src_ref=gown if p == 4 else part.at[p, 1 - core],
                dst_ref=garecv if p == 4 else arecv.at[p],
                send_sem=a_send.at[p],
                recv_sem=a_recv.at[p],
                device_id=partner,
                device_id_type=MESH,
            )
            for p in range(5)
        ]

        def far_copy(level, p, i, sending):
            other, device = peers[level](i)
            slot = me[level] if sending else other
            return pltpu.make_async_remote_copy(
                src_ref=gsends[level] if p == 4 else sends[level].at[p, other],
                dst_ref=grecvs[level].at[slot] if p == 4 else recvs[level].at[p, slot],
                send_sem=send_sems[level].at[p, other],
                recv_sem=recv_sems[level].at[p, slot],
                device_id=device,
                device_id_type=MESH,
            )

        def put(p, top, bottom):
            both = jnp.concatenate(
                [g.reshape(ndp * nseq, chunk // 2, -1) for g in (top, bottom)], axis=1
            ).astype(BF16)
            both = both.reshape(ndp // 2, 2, n2, inner, chunk, -1)
            for c in range(2):
                for x in range(ndp // 2):
                    for k in range(inner):
                        part[p, c, x * inner + k] = both[x, c, :, k]
            a_copies[p].start()

        def level1(p):
            a_copies[p].wait_recv()
            if p == 4:
                gsend1[...] = gown[...] + garecv[...]
                grecv1[me[0]] = gsend1[...]
            else:
                send1[p] = (part[p, core].astype(F32) + arecv[p].astype(F32)).astype(BF16)
                recv1[p, me[0]] = send1[p, me[0]]
            each(n1, lambda i: far_copy(0, p, i, True).start())

        def level2(p):
            each(n1, lambda i: far_copy(0, p, i, False).wait_recv())
            if p == 4:
                gsend2[...] = jnp.sum(grecv1[...], axis=0)
                grecv2[me[1]] = gsend2[...]
            else:
                send2[p] = jnp.sum(recv1[p].astype(F32), axis=0).astype(BF16)
                recv2[p, me[1]] = send2[p, me[1]]
            each(n2, lambda i: far_copy(1, p, i, True).start())

        def last(p):
            each(n2, lambda i: far_copy(1, p, i, False).wait_recv())
            if p == 4:
                gg_ref[...] = jnp.sum(grecv2[...], axis=0)[0:2] * factor
                return
            total = jnp.sum(recv2[p].astype(F32), axis=0) * factor
            r, w = chunk // 2, total.shape[1]
            b = 1 - p // 2
            for i in range(r):
                at = 4 * w * i + 2 * w * (1 - p % 2)
                wg_ref[b : b + 1, at : at + w] = total[i : i + 1]
                wg_ref[b : b + 1, at + w : at + 2 * w] = total[r + i : r + i + 1]
    else:

        def put(p, top, bottom):
            at = 2 * width * (1 - p % 2)
            b = 1 - p // 2
            wg_ref[b, :, at : at + width] = (top * factor).astype(BF16)
            wg_ref[b, :, at + width : at + 2 * width] = (bottom * factor).astype(BF16)

        def level1(p):
            pass

        level2 = last = level1

    cot_t = unfold(crecv[...].astype(F32))
    cot_tb = cot_t.astype(BF16)
    dms, dv = backward_value(cot_tb, st, w_ref, 1)
    dq, dk = backward_scores(dms, st)
    du, dg_t = backward_input(jnp.concatenate([dq, dk, dv], axis=1), st, g_t, w_ref, 1)
    msend[...] = fold(cot_t + du, nseq).astype(BF16)
    mrecv[seq] = msend[seq]
    m_start()
    put(0, dot(st["normed"], dv, 0, 0), dot(st["mixed"], cot_tb, 0, 0))
    put(1, dot(st["normed"], dq, 0, 0), dot(st["normed"], dk, 0, 0))
    level1(0)
    level1(1)

    m_arrive()
    cot_s = unfold(mrecv[...].astype(F32))
    cot_sb = cot_s.astype(BF16)
    dms, dv = backward_value(cot_sb, ss, w_ref, 0)
    put(2, dot(ss["normed"], dv, 0, 0), dot(ss["mixed"], cot_sb, 0, 0))
    level2(0)
    level2(1)
    dq, dk = backward_scores(dms, ss)
    put(3, dot(ss["normed"], dq, 0, 0), dot(ss["normed"], dk, 0, 0))
    level1(2)
    du, dg_s = backward_input(jnp.concatenate([dq, dk, dv], axis=1), ss, g_s, w_ref, 0)
    if fused:
        gown[...] = jnp.zeros_like(gown)
        gown[0:1, :] = dg_s
        gown[1:2, :] = dg_t
        a_copies[4].start()
    else:
        gg_ref[0:1, :] = dg_s * factor
        gg_ref[1:2, :] = dg_t * factor
    level1(3)
    ig_ref[...] = (cot_s + du).astype(BF16)
    level1(4)
    last(0)
    last(1)
    level2(2)
    level2(3)
    level2(4)
    last(2)
    last(3)
    last(4)
    if fused:
        for p in range(5):
            a_copies[p].wait_send()
            for level in range(2):
                each(sizes[level], lambda i: far_copy(level, p, i, True).wait_send())
    c_finish()
    m_finish()


def store_kernel(*refs):
    n = len(refs) // 2
    sem = refs[-1]
    copies = [pltpu.make_async_copy(refs[i], refs[n + i], sem.at[i]) for i in range(n)]
    for c in copies:
        c.start()
    for c in copies:
        c.wait()


def store_results(results):
    n = len(results)
    return pl.pallas_call(
        store_kernel,
        out_shape=tuple(jax.ShapeDtypeStruct(r.shape, r.dtype) for r in results),
        in_specs=[pl.BlockSpec(memory_space=pl.ANY)] * n,
        out_specs=(pl.BlockSpec(memory_space=pltpu.HBM),) * n,
        scratch_shapes=[pltpu.SemaphoreType.DMA((n,))],
        compiler_params=pltpu.CompilerParams(vmem_limit_bytes=1024 * 1024),
    )(*results)


def per_device(spatial_input, temporal_input, out_cotangent, weights, gains):
    ndp, nseq = lax.axis_size("dp"), lax.axis_size("seq")
    width = spatial_input.shape[-1]
    rows = spatial_input.shape[1] * spatial_input.shape[2]
    factor = 1.0 / math.sqrt(spatial_input.shape[0] * ndp * nseq * rows)
    per = rows // nseq
    wide = weights.shape[2]
    chunk_rows = width // (ndp * nseq)
    fused = ndp % 2 == 0 and chunk_rows * ndp * nseq == width and chunk_rows % 8 == 0
    message = pltpu.VMEM((nseq, 2 * per, width // 2), BF16)
    args = (
        spatial_input.reshape(rows, width),
        temporal_input.reshape(rows, width),
        out_cotangent.reshape(rows, width),
        weights,
        gains,
    )
    scratch = [pltpu.VMEM(a.shape, a.dtype) for a in args] + [pltpu.SemaphoreType.DMA((6,))]
    scratch += [message] * 4 + [pltpu.SemaphoreType.DMA((2, nseq))] * 2
    if fused:
        _, n1, n2 = groups(ndp, nseq)
        tile = (2 * chunk_rows, wide // 4)
        flat = pltpu.VMEM((8, width), F32)
        scratch += [
            pltpu.VMEM((4, 2, n1, n2) + tile, BF16),
            pltpu.VMEM((4, n1, n2) + tile, BF16),
            pltpu.VMEM((4, n1, n2) + tile, BF16),
            pltpu.VMEM((4, n1, n2) + tile, BF16),
            pltpu.VMEM((4, n2) + tile, BF16),
            pltpu.VMEM((4, n2) + tile, BF16),
            flat,
            flat,
            flat,
            pltpu.VMEM((n1, 8, width), F32),
            flat,
            pltpu.VMEM((n2, 8, width), F32),
            pltpu.SemaphoreType.DMA((5,)),
            pltpu.SemaphoreType.DMA((5,)),
            pltpu.SemaphoreType.DMA((5, n1)),
            pltpu.SemaphoreType.DMA((5, n1)),
            pltpu.SemaphoreType.DMA((5, n2)),
            pltpu.SemaphoreType.DMA((5, n2)),
        ]
        wg_shape = jax.ShapeDtypeStruct((2, chunk_rows * wide), F32)
    else:
        wg_shape = jax.ShapeDtypeStruct((2, width, wide), BF16)
    vmem = pl.BlockSpec(memory_space=pltpu.VMEM)
    results = pl.pallas_call(
        partial(kernel, ndp, nseq, fused, factor),
        out_shape=(
            jax.ShapeDtypeStruct((rows, width), BF16),
            wg_shape,
            jax.ShapeDtypeStruct((2, width), F32),
        ),
        in_specs=[pl.BlockSpec(memory_space=pltpu.HBM)] * 5,
        out_specs=(vmem,) * 3,
        scratch_shapes=scratch,
        compiler_params=pltpu.CompilerParams(
            collective_id=0, has_side_effects=True, vmem_limit_bytes=48 * 1024 * 1024
        ),
    )(*[pltpu.with_memory_space_constraint(a, pltpu.HBM) for a in args])
    input_grad, weight_grads, gain_grads = store_results(results) if fused else results
    if not fused:
        grid = weight_grads.reshape(2, ndp, nseq, -1)
        over = lax.psum_scatter(grid, "seq", scatter_dimension=2, tiled=True)
        over = lax.psum_scatter(
            over.reshape(2, ndp, -1), "dp", scatter_dimension=1, tiled=True
        )
        weight_grads = over.astype(F32).reshape(2, -1)
        gain_grads = lax.psum(gain_grads, ("dp", "seq"))
    return input_grad.reshape(spatial_input.shape), weight_grads, gain_grads


def solution(mesh):
    return jax.shard_map(
        per_device,
        mesh=mesh,
        in_specs=(
            P("dp", "seq", None, None),
            P("dp", "seq", None, None),
            P("dp", "seq", None, None),
            P(),
            P(),
        ),
        out_specs=(P("dp", "seq", None, None), P(None, ("dp", "seq")), P()),
        check_vma=False,
    )
```

```python
from functools import partial
import math

import jax
import jax.numpy as jnp
from jax import lax
from jax.experimental import pallas as pl
from jax.experimental.pallas import tpu as pltpu
from jax.sharding import PartitionSpec as P

HEADS = 4
F32 = jnp.float32
BF16 = jnp.bfloat16
MESH = pl.DeviceIdType.MESH


def dot(a, b, ca, cb):
    return lax.dot_general(a, b, (((ca,), (cb,)), ((), ())), preferred_element_type=F32)


def fold(x, parts):
    rows, width = x.shape
    x = x.reshape(parts, rows // parts, width)
    return jnp.concatenate([x[:, :, : width // 2], x[:, :, width // 2 :]], axis=1)


def unfold(x):
    parts, rows, half = x.shape
    x = jnp.concatenate([x[:, : rows // 2], x[:, rows // 2 :]], axis=2)
    return x.reshape(parts * (rows // 2), 2 * half)


def head_masks(rows, width):
    lane = lax.broadcasted_iota(jnp.int32, (rows, width), 1)
    size = width // HEADS
    return [(lane >= h * size) & (lane < (h + 1) * size) for h in range(HEADS)]


def spread(x, masks):
    zero = jnp.zeros_like(x)
    return jnp.concatenate([jnp.where(m, x, zero) for m in masks], axis=0)


def gather_heads(x, masks):
    rows = x.shape[0] // HEADS
    out = x[:rows]
    for h in range(1, HEADS):
        out = jnp.where(masks[h], x[h * rows : (h + 1) * rows], out)
    return out


def forward(u, gain, w_ref, block, same_group):
    rows, width = u.shape
    masks = head_masks(rows, width)
    scale = 1.0 / math.sqrt(width // HEADS)
    inv = lax.rsqrt(jnp.mean(u * u, axis=-1, keepdims=True) + 1e-06)
    unit = u * inv
    normed = (unit * gain).astype(BF16)
    packed = dot(normed, w_ref[block, :, : 3 * width], 1, 0)
    q, k, v = (packed[:, i * width : (i + 1) * width] for i in range(3))
    qs = spread(q, masks).astype(BF16)
    k = k.astype(BF16)
    v = v.astype(BF16)
    scores = dot(qs, k, 1, 1) * scale
    if same_group is not None:
        scores = jnp.where(same_group, scores, -1e30)
    e = jnp.exp(scores - jnp.max(scores, axis=-1, keepdims=True))
    probs = e / jnp.sum(e, axis=-1, keepdims=True)
    pb = probs.astype(BF16)
    mixed = gather_heads(dot(pb, v, 1, 0), masks).astype(BF16)
    return dict(unit=unit, inv=inv, normed=normed, qs=qs, k=k, v=v, probs=probs, pb=pb, mixed=mixed)


def backward_value(cot, s, w_ref, block):
    rows, width = cot.shape
    dmixed = dot(cot, w_ref[block, :, 3 * width :], 1, 1)
    dms = spread(dmixed, head_masks(rows, width)).astype(BF16)
    return dms, dot(s["pb"], dms, 0, 0).astype(BF16)


def backward_scores(dms, s):
    rows, width = s["k"].shape
    scale = 1.0 / math.sqrt(width // HEADS)
    dprobs = dot(dms, s["v"], 1, 1).astype(BF16).astype(F32)
    inner = jnp.sum(dprobs * s["probs"], axis=-1, keepdims=True)
    dscores = (s["probs"] * (dprobs - inner) * scale).astype(BF16)
    dq = gather_heads(dot(dscores, s["k"], 1, 0), head_masks(rows, width))
    dk = dot(dscores, s["qs"], 0, 0)
    return dq.astype(BF16), dk.astype(BF16)


def backward_input(dpacked, s, gain, w_ref, block):
    width = gain.shape[1]
    dn = dot(dpacked, w_ref[block, :, : 3 * width], 1, 1).astype(BF16).astype(F32)
    unit = s["unit"]
    dgain = jnp.sum(dn * unit, axis=0, keepdims=True)
    t = dn * gain
    du = s["inv"] * (t - unit * jnp.mean(unit * t, axis=-1, keepdims=True))
    return du, dgain


def each(n, body):
    if n <= 9:
        for i in range(1, n):
            body(i)
    else:
        pl.loop(1, n)(body)


def groups(ndp, nseq):
    inner = 2 if nseq % 2 == 0 else 1
    return inner, ndp // 2 * inner, nseq // inner


def kernel(ndp, nseq, fused, factor, *refs):
    ig_ref, wg_ref, gg_ref = refs[5:8]
    sp_ref, tp_ref, cot_ref, w_ref, g_ref, load_sem = refs[8:14]
    csend, crecv, msend, mrecv, x_send, x_recv = refs[14:20]
    sp_hbm, tp_hbm, cot_hbm, w_hbm, g_hbm = refs[:5]
    pairs = [
        (cot_hbm, cot_ref),
        (tp_hbm, tp_ref),
        (g_hbm, g_ref),
        (w_hbm.at[1], w_ref.at[1]),
        (sp_hbm, sp_ref),
        (w_hbm.at[0], w_ref.at[0]),
    ]
    loads = [pltpu.make_async_copy(s, d, load_sem.at[i]) for i, (s, d) in enumerate(pairs)]
    for load in loads:
        load.start()
    dp, seq = lax.axis_index("dp"), lax.axis_index("seq")
    rows, width = cot_ref.shape
    per = rows // nseq
    inner, n1, n2 = groups(ndp, nseq)
    core = lax.rem(dp, 2)
    partner = (dp + 1 - 2 * core, seq)
    far = lax.div(dp, 2)
    z = lax.div(seq, inner)
    y = seq - z * inner
    me = (far * inner + y, z)

    def peer1(i):
        other = lax.rem(me[0] + i, n1)
        x = lax.div(other, inner)
        return other, (2 * x + core, z * inner + other - x * inner)

    def peer2(i):
        other = lax.rem(z + i, n2)
        return other, (dp, other * inner + y)

    def near(i):
        other = lax.rem(seq + i, nseq)
        return other, (dp, other)

    barrier = pltpu.get_barrier_semaphore()

    def greet(device):
        pl.semaphore_signal(barrier, inc=1, device_id=device, device_id_type=MESH)

    each(nseq, lambda i: greet(near(i)[1]))
    greeted = nseq - 1
    if fused:
        greet(partner)
        nx = ndp // 2
        for k in range(inner):
            each(nx, lambda i: greet((2 * lax.rem(far + i, nx) + core, z * inner + k)))
        greeted += 1 + inner * (nx - 1)

    def exchange(level, send, recv):
        def copy(i, slot):
            other, device = near(i)
            return pltpu.make_async_remote_copy(
                src_ref=send.at[other],
                dst_ref=recv.at[slot(other)],
                send_sem=x_send.at[level, other],
                recv_sem=x_recv.at[level, slot(other)],
                device_id=device,
                device_id_type=MESH,
            )

        def start():
            each(nseq, lambda i: copy(i, lambda other: seq).start())

        def arrive():
            each(nseq, lambda i: copy(i, lambda other: other).wait_recv())

        def finish():
            each(nseq, lambda i: copy(i, lambda other: seq).wait_send())

        return start, arrive, finish

    c_start, c_arrive, c_finish = exchange(0, csend, crecv)
    m_start, m_arrive, m_finish = exchange(1, msend, mrecv)

    loads[0].wait()
    csend[...] = fold(cot_ref[...].astype(F32), nseq).astype(BF16)
    crecv[seq] = csend[seq]

    frames = rows // per
    at = lax.broadcasted_iota(jnp.int32, (rows, rows), 0)
    frm = lax.broadcasted_iota(jnp.int32, (rows, rows), 1)
    pick = (frm == lax.rem(at, per) * frames + lax.div(at, per)).astype(F32).astype(BF16)
    loads[1].wait()
    ut = dot(pick, tp_ref[...], 1, 0)
    ri = lax.broadcasted_iota(jnp.int32, (HEADS * rows, rows), 0)
    ci = lax.broadcasted_iota(jnp.int32, (HEADS * rows, rows), 1)
    same = lax.rem(ri, per) == lax.rem(ci, per)
    loads[2].wait()
    loads[3].wait()
    g_t, g_s = g_ref[1:2, :], g_ref[0:1, :]
    st = forward(ut, g_t, w_ref, 1, same)

    pl.semaphore_wait(barrier, greeted)
    c_start()
    loads[4].wait()
    loads[5].wait()
    ss = forward(sp_ref[...].astype(F32), g_s, w_ref, 0, None)
    c_arrive()

    if fused:
        part, arecv, send1, recv1, send2, recv2 = refs[20:26]
        gown, garecv, gsend1, grecv1, gsend2, grecv2 = refs[26:32]
        a_send, a_recv, s_send1, s_recv1, s_send2, s_recv2 = refs[32:38]
        chunk = part.shape[4]
        sends = (send1, send2)
        recvs = (recv1, recv2)
        gsends = (gsend1, gsend2)
        grecvs = (grecv1, grecv2)
        send_sems = (s_send1, s_send2)
        recv_sems = (s_recv1, s_recv2)
        peers = (peer1, peer2)
        sizes = (n1, n2)

        a_copies = [
            pltpu.make_async_remote_copy(
                src_ref=gown if p == 4 else part.at[p, 1 - core],
                dst_ref=garecv if p == 4 else arecv.at[p],
                send_sem=a_send.at[p],
                recv_sem=a_recv.at[p],
                device_id=partner,
                device_id_type=MESH,
            )
            for p in range(5)
        ]

        def far_copy(level, p, i, sending):
            other, device = peers[level](i)
            slot = me[level] if sending else other
            return pltpu.make_async_remote_copy(
                src_ref=gsends[level] if p == 4 else sends[level].at[p, other],
                dst_ref=grecvs[level].at[slot] if p == 4 else recvs[level].at[p, slot],
                send_sem=send_sems[level].at[p, other],
                recv_sem=recv_sems[level].at[p, slot],
                device_id=device,
                device_id_type=MESH,
            )

        def put(p, top, bottom):
            both = jnp.concatenate(
                [g.reshape(ndp * nseq, chunk // 2, -1) for g in (top, bottom)], axis=1
            ).astype(BF16)
            both = both.reshape(ndp // 2, 2, n2, inner, chunk, -1)
            for c in range(2):
                for x in range(ndp // 2):
                    for k in range(inner):
                        part[p, c, x * inner + k] = both[x, c, :, k]
            a_copies[p].start()

        def level1(p):
            a_copies[p].wait_recv()
            if p == 4:
                gsend1[...] = gown[...] + garecv[...]
                grecv1[me[0]] = gsend1[...]
            else:
                send1[p] = (part[p, core].astype(F32) + arecv[p].astype(F32)).astype(BF16)
                recv1[p, me[0]] = send1[p, me[0]]
            each(n1, lambda i: far_copy(0, p, i, True).start())

        def level2(p):
            each(n1, lambda i: far_copy(0, p, i, False).wait_recv())
            if p == 4:
                gsend2[...] = jnp.sum(grecv1[...], axis=0)
                grecv2[me[1]] = gsend2[...]
            else:
                send2[p] = jnp.sum(recv1[p].astype(F32), axis=0).astype(BF16)
                recv2[p, me[1]] = send2[p, me[1]]
            each(n2, lambda i: far_copy(1, p, i, True).start())

        def last(p):
            each(n2, lambda i: far_copy(1, p, i, False).wait_recv())
            if p == 4:
                gg_ref[...] = jnp.sum(grecv2[...], axis=0)[0:2] * factor
                return
            total = jnp.sum(recv2[p].astype(F32), axis=0) * factor
            r, w = chunk // 2, total.shape[1]
            b = 1 - p // 2
            for i in range(r):
                at = 4 * w * i + 2 * w * (1 - p % 2)
                wg_ref[b : b + 1, at : at + w] = total[i : i + 1]
                wg_ref[b : b + 1, at + w : at + 2 * w] = total[r + i : r + i + 1]
    else:

        def put(p, top, bottom):
            at = 2 * width * (1 - p % 2)
            b = 1 - p // 2
            wg_ref[b, :, at : at + width] = (top * factor).astype(BF16)
            wg_ref[b, :, at + width : at + 2 * width] = (bottom * factor).astype(BF16)

        def level1(p):
            pass

        level2 = last = level1

    cot_t = unfold(crecv[...].astype(F32))
    cot_tb = cot_t.astype(BF16)
    dms, dv = backward_value(cot_tb, st, w_ref, 1)
    dq, dk = backward_scores(dms, st)
    du, dg_t = backward_input(jnp.concatenate([dq, dk, dv], axis=1), st, g_t, w_ref, 1)
    msend[...] = fold(cot_t + du, nseq).astype(BF16)
    mrecv[seq] = msend[seq]
    m_start()
    put(0, dot(st["normed"], dv, 0, 0), dot(st["mixed"], cot_tb, 0, 0))
    put(1, dot(st["normed"], dq, 0, 0), dot(st["normed"], dk, 0, 0))
    level1(0)
    level1(1)

    m_arrive()
    cot_s = unfold(mrecv[...].astype(F32))
    cot_sb = cot_s.astype(BF16)
    dms, dv = backward_value(cot_sb, ss, w_ref, 0)
    put(2, dot(ss["normed"], dv, 0, 0), dot(ss["mixed"], cot_sb, 0, 0))
    dq, dk = backward_scores(dms, ss)
    put(3, dot(ss["normed"], dq, 0, 0), dot(ss["normed"], dk, 0, 0))
    level1(2)
    du, dg_s = backward_input(jnp.concatenate([dq, dk, dv], axis=1), ss, g_s, w_ref, 0)
    if fused:
        gown[...] = jnp.zeros_like(gown)
        gown[0:1, :] = dg_s
        gown[1:2, :] = dg_t
        a_copies[4].start()
    else:
        gg_ref[0:1, :] = dg_s * factor
        gg_ref[1:2, :] = dg_t * factor
    level1(3)
    level1(4)
    level2(0)
    level2(1)
    ig_ref[...] = (cot_s + du).astype(BF16)
    level2(2)
    level2(3)
    level2(4)
    last(0)
    last(1)
    last(2)
    last(3)
    last(4)
    if fused:
        for p in range(5):
            a_copies[p].wait_send()
            for level in range(2):
                each(sizes[level], lambda i: far_copy(level, p, i, True).wait_send())
    c_finish()
    m_finish()


def store_kernel(*refs):
    n = len(refs) // 2
    sem = refs[-1]
    copies = [pltpu.make_async_copy(refs[i], refs[n + i], sem.at[i]) for i in range(n)]
    for c in copies:
        c.start()
    for c in copies:
        c.wait()


def store_results(results):
    n = len(results)
    return pl.pallas_call(
        store_kernel,
        out_shape=tuple(jax.ShapeDtypeStruct(r.shape, r.dtype) for r in results),
        in_specs=[pl.BlockSpec(memory_space=pl.ANY)] * n,
        out_specs=(pl.BlockSpec(memory_space=pltpu.HBM),) * n,
        scratch_shapes=[pltpu.SemaphoreType.DMA((n,))],
        compiler_params=pltpu.CompilerParams(vmem_limit_bytes=1024 * 1024),
    )(*results)


def per_device(spatial_input, temporal_input, out_cotangent, weights, gains):
    ndp, nseq = lax.axis_size("dp"), lax.axis_size("seq")
    width = spatial_input.shape[-1]
    rows = spatial_input.shape[1] * spatial_input.shape[2]
    factor = 1.0 / math.sqrt(spatial_input.shape[0] * ndp * nseq * rows)
    per = rows // nseq
    wide = weights.shape[2]
    chunk_rows = width // (ndp * nseq)
    fused = ndp % 2 == 0 and chunk_rows * ndp * nseq == width and chunk_rows % 8 == 0
    message = pltpu.VMEM((nseq, 2 * per, width // 2), BF16)
    args = (
        spatial_input.reshape(rows, width),
        temporal_input.reshape(rows, width),
        out_cotangent.reshape(rows, width),
        weights,
        gains,
    )
    scratch = [pltpu.VMEM(a.shape, a.dtype) for a in args] + [pltpu.SemaphoreType.DMA((6,))]
    scratch += [message] * 4 + [pltpu.SemaphoreType.DMA((2, nseq))] * 2
    if fused:
        _, n1, n2 = groups(ndp, nseq)
        tile = (2 * chunk_rows, wide // 4)
        flat = pltpu.VMEM((8, width), F32)
        scratch += [
            pltpu.VMEM((4, 2, n1, n2) + tile, BF16),
            pltpu.VMEM((4, n1, n2) + tile, BF16),
            pltpu.VMEM((4, n1, n2) + tile, BF16),
            pltpu.VMEM((4, n1, n2) + tile, BF16),
            pltpu.VMEM((4, n2) + tile, BF16),
            pltpu.VMEM((4, n2) + tile, BF16),
            flat,
            flat,
            flat,
            pltpu.VMEM((n1, 8, width), F32),
            flat,
            pltpu.VMEM((n2, 8, width), F32),
            pltpu.SemaphoreType.DMA((5,)),
            pltpu.SemaphoreType.DMA((5,)),
            pltpu.SemaphoreType.DMA((5, n1)),
            pltpu.SemaphoreType.DMA((5, n1)),
            pltpu.SemaphoreType.DMA((5, n2)),
            pltpu.SemaphoreType.DMA((5, n2)),
        ]
        wg_shape = jax.ShapeDtypeStruct((2, chunk_rows * wide), F32)
    else:
        wg_shape = jax.ShapeDtypeStruct((2, width, wide), BF16)
    vmem = pl.BlockSpec(memory_space=pltpu.VMEM)
    results = pl.pallas_call(
        partial(kernel, ndp, nseq, fused, factor),
        out_shape=(
            jax.ShapeDtypeStruct((rows, width), BF16),
            wg_shape,
            jax.ShapeDtypeStruct((2, width), F32),
        ),
        in_specs=[pl.BlockSpec(memory_space=pltpu.HBM)] * 5,
        out_specs=(vmem,) * 3,
        scratch_shapes=scratch,
        compiler_params=pltpu.CompilerParams(
            collective_id=0, has_side_effects=True, vmem_limit_bytes=48 * 1024 * 1024
        ),
    )(*[pltpu.with_memory_space_constraint(a, pltpu.HBM) for a in args])
    input_grad, weight_grads, gain_grads = store_results(results) if fused else results
    if not fused:
        grid = weight_grads.reshape(2, ndp, nseq, -1)
        over = lax.psum_scatter(grid, "seq", scatter_dimension=2, tiled=True)
        over = lax.psum_scatter(
            over.reshape(2, ndp, -1), "dp", scatter_dimension=1, tiled=True
        )
        weight_grads = over.astype(F32).reshape(2, -1)
        gain_grads = lax.psum(gain_grads, ("dp", "seq"))
    return input_grad.reshape(spatial_input.shape), weight_grads, gain_grads


def solution(mesh):
    return jax.shard_map(
        per_device,
        mesh=mesh,
        in_specs=(
            P("dp", "seq", None, None),
            P("dp", "seq", None, None),
            P("dp", "seq", None, None),
            P(),
            P(),
        ),
        out_specs=(P("dp", "seq", None, None), P(None, ("dp", "seq")), P()),
        check_vma=False,
    )
```
